32 devices in a mesh: groups: 2 (over y), cand: 4 (over x, core), hist: 4 (over z).
Axes of the slice: x: 2, y: 2, z: 4, core: 2. Of those that a mesh axis runs over, the one named last changes fastest.
Arguments:
- cand_feats: bfloat16 [2048, 256], P(('groups', 'cand')), parts along dimension 0, may hold values from -6 to 6
- cat_table: bfloat16 [4, 256], P('groups'), parts along dimension 0, may hold values from -5 to 5
- cand_cat: int32 [2048], P(('groups', 'cand')), parts along dimension 0, may hold values from 0 to 1
- cand_blocks: int32 [2048, 16], P(('groups', 'cand')), parts along dimension 0, may hold values from 0 to 127, as said below
- cand_count: int32 [2048], P(('groups', 'cand')), parts along dimension 0, may hold values from 1 to 16
- keys: bfloat16 [32768, 256], P(('groups', 'cand', 'hist')), parts along dimension 0, may hold values from -6 to 6
- values: bfloat16 [32768, 256], P(('groups', 'cand', 'hist')), parts along dimension 0, may hold values from -6 to 6
- w_query: bfloat16 [256, 256], replicated, may hold values from -0.375 to 0.375
- norm_gain: float32 [256], replicated, may hold values from 0.25 to 1.75
- w_up: bfloat16 [256, 1024], replicated, may hold values from -0.375 to 0.375
- w_down: bfloat16 [1024, 256], replicated, may hold values from -0.1875 to 0.1875
Outputs:
- ranked: bfloat16 [2048, 256], P(('groups', 'cand')), parts along dimension 0
The draws below stay inside these ranges and needn't reach their ends.
There are 2 independent parts, one for each index of `groups`. The reference program is written for one: setup_inputs(seed, part) draws one part's arguments, and reference() takes and returns one part's arrays. A program takes and returns all parts, laid end to end along the dimension named above; an argument that names none is the same for every part. Nothing has to cross between parts.
Inputs may be any that keep to these rules, and one draw needn't show every extreme that they name: `cand_blocks`: block b has category b % 2; every block a candidate lists has the candidate's category, and the 16 ids in one row are distinct. Some candidate uses all 16 slots and some only one.
All inputs are finite; a program needn't handle non-finite values.
Results may differ from the reference program's by a relative error of at most 0.0055.
Values may be sent and summed in bfloat16 or wider, within the bound.
No kernel may reach another device: no remote copies, remote signals or barrier semaphores. Data moves between devices by JAX's collectives and lax.ppermute only.
A program may use at most 64 MiB of HBM per device.

```python
import math
import jax
import jax.numpy as jnp
from jax import lax

D = 256
HEADS = 4
HEAD_DIM = 64
FFN = 1024
BLOCK = 128
LIST = 16
CATS = 2
CANDS = 1024
NB = 128
BEHAV = 16384
CAT_BLOCKS = 64


def category_draw(key):
    return jax.random.randint(jax.random.fold_in(key, 11), (CANDS,), 0, CATS, dtype=jnp.int32)


def draw_cand_cat(key, part):
    return category_draw(key)


def draw_cand_blocks(key, part):
    category = category_draw(key)
    ranks = jax.random.randint(jax.random.fold_in(key, 15), (CANDS, CAT_BLOCKS), 0, 4096, dtype=jnp.int32)
    scores = ranks * CAT_BLOCKS + jnp.arange(CAT_BLOCKS, dtype=jnp.int32)[None, :]
    within = lax.top_k(scores, LIST)[1].astype(jnp.int32)
    return (category[:, None] + CATS * within).astype(jnp.int32)


def draw_cand_count(key, part):
    counts = jax.random.randint(jax.random.fold_in(key, 14), (CANDS,), 1, LIST + 1, dtype=jnp.int32)
    position = jnp.arange(CANDS, dtype=jnp.int32)
    counts = jnp.where(position % 64 == 0, LIST, counts)
    counts = jnp.where(position % 64 == 1, 1, counts)
    return counts.astype(jnp.int32)


def steps_of(own_key, shape, cuts, low, largest):
    level, own = 1.0, jax.random.fold_in(own_key, 6)
    for dim, parts in cuts:
        draws = jnp.exp(jax.random.uniform(jax.random.fold_in(own, dim), (parts,), jnp.float32, low / len(cuts), largest / len(cuts)))
        level = level * jnp.repeat(draws, shape[dim] // parts).reshape([-1 if axis == dim else 1 for axis in range(len(shape))])
    return level


def noise(key, extent, scale, reach, split=(), kind=jnp.bfloat16):
    values = scale * jax.random.normal(key, extent, jnp.float32)
    if split:
        values = values * steps_of(key, extent, split, -0.22, 0.18)
    return jnp.clip(values, -reach, reach).astype(kind)


def setup_inputs(seed: int = 0, part: int = 0) -> dict:
    seeds = jax.random.split(jax.random.key(seed), 12)
    part_keys = jax.random.split(jax.random.fold_in(seeds[11], part), 12)
    return {
        "cand_feats": noise(part_keys[0], (CANDS, D), 1.0, 6.0, ((0, 4),)),
        "cat_table": noise(part_keys[1], (CATS, D), 0.7, 5.0),
        "cand_cat": draw_cand_cat(jax.random.fold_in(jax.random.fold_in(seeds[11], part), 71), part),
        "cand_blocks": draw_cand_blocks(jax.random.fold_in(jax.random.fold_in(seeds[11], part), 71), part),
        "cand_count": draw_cand_count(jax.random.fold_in(jax.random.fold_in(seeds[11], part), 71), part),
        "keys": noise(part_keys[5], (BEHAV, D), 1.0, 6.0, ((0, 16),)),
        "values": noise(part_keys[6], (BEHAV, D), 1.0, 6.0, ((0, 16),)),
        "w_query": noise(seeds[7], (D, D), D ** -0.5, 0.375),
        "norm_gain": jnp.clip(1.0 + 0.15 * jax.random.normal(seeds[8], (D,), jnp.float32), 0.25, 1.75),
        "w_up": noise(seeds[9], (D, FFN), D ** -0.5, 0.375),
        "w_down": noise(seeds[10], (FFN, D), FFN ** -0.5, 0.1875),
    }


def reference(cand_feats, cat_table, cand_cat, cand_blocks, cand_count, keys, values, w_query, norm_gain, w_up, w_down):
    onehot = (cand_cat[:, None] == jnp.arange(CATS, dtype=jnp.int32)[None, :]).astype(jnp.bfloat16)
    embedded = jnp.dot(onehot, cat_table, preferred_element_type=jnp.float32)
    query_input = (cand_feats.astype(jnp.float32) + embedded).astype(jnp.bfloat16)
    query = jnp.dot(query_input, w_query, preferred_element_type=jnp.float32).astype(jnp.bfloat16)
    query = query.reshape(CANDS, HEADS, HEAD_DIM)
    key_blocks = keys.reshape(NB, BLOCK, HEADS, HEAD_DIM)
    value_blocks = values.reshape(NB, BLOCK, HEADS, HEAD_DIM)
    score_scale = 1.0 / math.sqrt(HEAD_DIM)
    row_block = math.gcd(CANDS, 64)

    def attend(inputs_block):
        query_rows, block_ids, counts = inputs_block
        key_rows = key_blocks[block_ids].astype(jnp.float32)
        value_rows = value_blocks[block_ids].astype(jnp.float32)
        scores = jnp.einsum('rhd,rlbhd->rlbh', query_rows.astype(jnp.float32), key_rows) * score_scale
        slot_live = (jnp.arange(LIST, dtype=jnp.int32)[None, :] < counts[:, None]).astype(jnp.float32)
        weights_bf = (jax.nn.silu(scores) * slot_live[:, :, None, None]).astype(jnp.bfloat16)
        return jnp.einsum('rlbh,rlbhd->rhd', weights_bf.astype(jnp.float32), value_rows)
    attended = lax.map(attend, (query.reshape(-1, row_block, HEADS, HEAD_DIM), cand_blocks.reshape(-1, row_block, LIST), cand_count.reshape(-1, row_block)))
    attended = attended.reshape(CANDS, D)
    mean_square = lax.optimization_barrier(jnp.mean(attended * attended, axis=-1, keepdims=True))
    normed = (attended * lax.rsqrt(mean_square + 1e-06) * norm_gain).astype(jnp.bfloat16)
    hidden = jax.nn.silu(jnp.dot(normed, w_up, preferred_element_type=jnp.float32)).astype(jnp.bfloat16)
    result = cand_feats.astype(jnp.float32) + jnp.dot(hidden, w_down, preferred_element_type=jnp.float32)
    return result.astype(jnp.bfloat16)
```

```python
import functools
import math

import jax
import jax.numpy as jnp
from jax import lax
from jax.experimental import pallas as pl
from jax.experimental.pallas import tpu as pltpu
from jax.sharding import PartitionSpec as P

HEADS = 4
BLOCK = 128
CATS = 2
CORES = 2
BF16 = jnp.bfloat16
F32 = jnp.float32


def contract_rows(lhs, rhs):
    return lax.dot_general(lhs, rhs, (((0,), (0,)), ((), ())), preferred_element_type=F32)


def contract_lanes(lhs, rhs):
    return lax.dot_general(lhs, rhs, (((1,), (1,)), ((), ())), preferred_element_type=F32)


def pack_kernel(bases_ref, lists_ref, cat_ref, count_ref, out_ref, *, pairs, pieces):
    lists = lists_ref[...]
    cat = cat_ref[...]
    slot = lax.broadcasted_iota(jnp.int32, lists.shape, 0)
    live = jnp.where(slot < count_ref[...], lists, -1)
    width = lists.shape[1]
    row = lax.broadcasted_iota(jnp.int32, (out_ref.shape[1], width), 0)
    for target in range(out_ref.shape[0]):
        packed = jnp.where(row == pieces * pairs, cat, 0)
        for piece in range(pieces):
            base = bases_ref[target * pieces + piece]
            for pair in range(pairs):
                hit = jnp.where(live == base + CATS * pair + cat, 1, 0)
                hit = jnp.max(hit, axis=0, keepdims=True)
                packed = jnp.where(row == piece * pairs + pair, hit, packed)
        out_ref[target] = packed.astype(F32).astype(BF16)


def attend_kernel(
    feats_ref,
    pack_ref,
    table_ref,
    wq_ref,
    *refs,
    pairs,
    pieces,
):
    kv_refs = refs[: 2 * pieces]
    out_ref, mask_ref, kst_ref, vst_ref = refs[2 * pieces :]
    rows, width = feats_ref.shape
    head = width // HEADS
    tile = 2 * head
    keys = pieces * pairs * BLOCK
    pack = pack_ref[...]
    cat = pack[pieces * pairs : pieces * pairs + 1, :].astype(F32)
    cat_id = lax.broadcasted_iota(jnp.int32, (CATS, rows), 0).astype(F32)
    onehot = jnp.where(cat_id == cat, 1.0, 0.0).astype(BF16)
    embedded = contract_rows(onehot, table_ref[...])
    side = lax.broadcasted_iota(jnp.int32, (CATS, tile), 1) // head
    own_side = side == lax.broadcasted_iota(jnp.int32, (CATS, tile), 0)
    keep_even = contract_rows(onehot, jnp.where(own_side, 1.0, 0.0).astype(BF16))
    keep_odd = 1.0 - keep_even
    query_in = (feats_ref[...].astype(F32) + embedded).astype(BF16)
    query = jnp.dot(query_in, wq_ref[...], preferred_element_type=F32).astype(BF16).astype(F32)
    query = query * (0.5 / math.sqrt(head))
    pair_id = lax.broadcasted_iota(jnp.int32, (pack.shape[0], keys), 0)
    key_pair = lax.broadcasted_iota(jnp.int32, (pack.shape[0], keys), 1) // BLOCK
    expand = jnp.where(pair_id == key_pair, 1.0, 0.0).astype(BF16)
    mask_ref[...] = contract_rows(pack, expand).astype(BF16)

    low = lax.broadcasted_iota(jnp.int32, (BLOCK, tile), 1) < head
    for piece in range(pieces):
        for source, target in ((kv_refs[2 * piece], kst_ref), (kv_refs[2 * piece + 1], vst_ref)):
            for pair in range(pairs):
                at = (piece * pairs + pair) * BLOCK
                for t in range(HEADS // 2):
                    lanes = slice(t * tile, (t + 1) * tile)
                    even = source[2 * pair * BLOCK : (2 * pair + 1) * BLOCK, lanes]
                    odd = source[(2 * pair + 1) * BLOCK : (2 * pair + 2) * BLOCK, lanes]
                    odd = jnp.concatenate([odd[:, head:], odd[:, :head]], axis=1)
                    target[2 * t, at : at + BLOCK, :] = jnp.where(low, even, odd)
                    target[2 * t + 1, at : at + BLOCK, :] = jnp.where(low, odd, even)

    low_rows = lax.broadcasted_iota(jnp.int32, (rows, tile), 1) < head
    chunk = 2 * BLOCK
    for t in range(HEADS // 2):
        straight = query[:, t * tile : (t + 1) * tile]
        turned = pltpu.roll(straight, head, 1)
        sums = []
        for h in range(2):
            if h == 0:
                stacked = jnp.where(low_rows, straight, turned) * keep_even
            else:
                stacked = jnp.where(low_rows, turned, straight) * keep_odd
            stacked = stacked.astype(BF16)
            total = jnp.zeros((rows, tile), F32)
            for c in range(keys // chunk):
                span = slice(c * chunk, (c + 1) * chunk)
                half = contract_lanes(stacked, kst_ref[2 * t + h, span, :])
                weight = (half + half * jnp.tanh(half)).astype(BF16) * mask_ref[:, span]
                total += jnp.dot(
                    weight, vst_ref[2 * t + h, span, :], preferred_element_type=F32
                )
            total = total * (keep_even if h == 0 else keep_odd)
            sums.append(total + pltpu.roll(total, head, 1))
        out_ref[:, t * tile : (t + 1) * tile] = jnp.where(low_rows, sums[0], sums[1]).astype(
            out_ref.dtype
        )


def finish_kernel(mine_ref, theirs_ref, feats_ref, gain_ref, up_ref, down_ref, out_ref):
    attended = mine_ref[...].astype(F32) + theirs_ref[...].astype(F32)
    mean_square = jnp.mean(attended * attended, axis=-1, keepdims=True)
    normed = (attended * lax.rsqrt(mean_square + 1e-06) * gain_ref[...]).astype(BF16)
    half = 0.5 * jnp.dot(normed, up_ref[...], preferred_element_type=F32)
    hidden = (half + half * jnp.tanh(half)).astype(BF16)
    result = feats_ref[...].astype(F32) + jnp.dot(
        hidden, down_ref[...], preferred_element_type=F32
    )
    out_ref[...] = result.astype(BF16)


def in_vmem(count):
    return [pl.BlockSpec(memory_space=pltpu.VMEM)] * count


def shards(
    cand_feats,
    cat_table,
    cand_cat,
    cand_blocks,
    cand_count,
    keys,
    values,
    w_query,
    norm_gain,
    w_up,
    w_down,
):
    rows, width = cand_feats.shape
    piece_rows = keys.shape[0]
    blocks_here = piece_rows // BLOCK
    pairs = blocks_here // CATS
    cand_size = lax.axis_size("cand")
    hist_size = lax.axis_size("hist")
    chips = cand_size // CORES
    me = lax.axis_index("cand")
    hist = lax.axis_index("hist")
    core = me % CORES
    places = range(cand_size * hist_size)

    def moved(array, chip_step, hist_flip):
        route = []
        for place in places:
            c, z = divmod(place, hist_size)
            route.append((place, (c + CORES * chip_step) % cand_size * hist_size + (z ^ hist_flip)))
        return lax.ppermute(array, ("cand", "hist"), route)

    def swapped(array):
        return lax.ppermute(array, "cand", [(i, i ^ 1) for i in range(cand_size)])

    def bases_of(chip):
        mine = ((chip * CORES + core) * hist_size + hist) * blocks_here
        other = ((chip * CORES + (1 - core)) * hist_size + hist) * blocks_here
        return [mine, other]

    feats_in = [cand_feats] + [moved(cand_feats, s, 0) for s in range(1, chips)]
    keys_pair = (keys, swapped(keys))
    values_pair = (values, swapped(values))

    bases = []
    for s in range(chips):
        bases += bases_of((me // CORES + s) % chips)
    bases = jnp.stack(bases).astype(jnp.int32)
    pack_rows = -(-(CORES * pairs + 1) // 16) * 16
    packs = pl.pallas_call(
        functools.partial(pack_kernel, pairs=pairs, pieces=CORES),
        out_shape=jax.ShapeDtypeStruct((chips, pack_rows, rows), BF16),
        in_specs=[pl.BlockSpec(memory_space=pltpu.SMEM)] + in_vmem(3),
        out_specs=pl.BlockSpec(memory_space=pltpu.VMEM),
        name="pack",
    )(bases, cand_blocks.T, cand_cat[None, :], cand_count[None, :])
    packs_in = [packs[0]] + [moved(packs[s], s, 0) for s in range(1, chips)]

    def attend(feats, pack):
        span = CORES * pairs * BLOCK
        return pl.pallas_call(
            functools.partial(attend_kernel, pairs=pairs, pieces=CORES),
            out_shape=jax.ShapeDtypeStruct((rows, width), BF16),
            in_specs=in_vmem(4 + 2 * CORES),
            out_specs=pl.BlockSpec(memory_space=pltpu.VMEM),
            scratch_shapes=[
                pltpu.VMEM((rows, span), BF16),
                pltpu.VMEM((HEADS, span, width // HEADS * 2), BF16),
                pltpu.VMEM((HEADS, span, width // HEADS * 2), BF16),
            ],
            cost_estimate=pl.CostEstimate(
                flops=4 * rows * span * width * 2, bytes_accessed=3 << 20, transcendentals=0
            ),
            name="attend",
        )(feats, pack, cat_table, w_query, keys_pair[0], values_pair[0], keys_pair[1], values_pair[1])

    partial = attend(feats_in[0], packs_in[0])
    for s in range(1, chips):
        away = attend(feats_in[s], packs_in[s])
        back = moved(away, chips - s, 0)
        partial = (partial.astype(F32) + back.astype(F32)).astype(BF16)

    flips = [2**k - 1 for k in range(1, hist_size.bit_length())]
    for flip in flips[:-1]:
        arrived = moved(partial, 0, flip)
        partial = (partial.astype(F32) + arrived.astype(F32)).astype(BF16)
    arrived = moved(partial, 0, flips[-1])
    return pl.pallas_call(
        finish_kernel,
        out_shape=jax.ShapeDtypeStruct((rows, width), BF16),
        in_specs=in_vmem(6),
        out_specs=pl.BlockSpec(memory_space=pltpu.VMEM),
        name="finish",
    )(partial, arrived, cand_feats, norm_gain[None, :], w_up, w_down)


def solution(mesh):
    in_specs = (
        P(("groups", "cand"), None),
        P("groups", None),
        P(("groups", "cand")),
        P(("groups", "cand"), None),
        P(("groups", "cand")),
        P(("groups", "cand", "hist"), None),
        P(("groups", "cand", "hist"), None),
        P(),
        P(),
        P(),
        P(),
    )
    out_specs = P(("groups", "cand"), None)
    return jax.shard_map(shards, mesh=mesh, in_specs=in_specs, out_specs=out_specs, check_vma=False)
```

```python
import functools
import math

import jax
import jax.numpy as jnp
from jax import lax
from jax.experimental import pallas as pl
from jax.experimental.pallas import tpu as pltpu
from jax.sharding import PartitionSpec as P


HEADS = 4
BLOCK = 128
CATS = 2
CORES = 2
BF16 = jnp.bfloat16
F32 = jnp.float32


def contract_rows(lhs, rhs):
    return lax.dot_general(lhs, rhs, (((0,), (0,)), ((), ())), preferred_element_type=F32)


def contract_lanes(lhs, rhs):
    return lax.dot_general(lhs, rhs, (((1,), (1,)), ((), ())), preferred_element_type=F32)


def start_kernel(*refs):
    half = len(refs) // 2
    copies = [
        pltpu.make_async_copy(source, target, refs[-1].at[i])
        for i, (source, target) in enumerate(zip(refs[:half], refs[half:]))
    ]
    for copy in copies:
        copy.start()
    for copy in copies:
        copy.wait()


def pair_rows(refs, lanes):
    even, odd = [], []
    for ref in refs:
        for start in range(0, ref.shape[0], CATS * BLOCK):
            even.append(ref[start : start + BLOCK, lanes])
            odd.append(ref[start + BLOCK : start + CATS * BLOCK, lanes])
    return even, odd


def attend_kernel(feats_ref, lists_ref, count_ref, table_ref, wq_ref, *refs, first_blocks):
    bases = first_blocks()
    pieces = len(bases)
    key_refs, value_refs = refs[:pieces], refs[pieces : 2 * pieces]
    out_ref, mask_ref, weight_ref = refs[2 * pieces :]
    rows, width = feats_ref.shape
    head = width // HEADS
    tile = 2 * head
    both = CATS * tile
    total_keys = weight_ref.shape[1]
    pair_count = total_keys // BLOCK

    lists = lists_ref[...]
    cat = lax.rem(lists[:1, :], CATS)
    slot = lax.broadcasted_iota(jnp.int32, lists.shape, 0)
    live = jnp.where(slot < count_ref[...], lists - cat, -CATS)
    pack_row = lax.broadcasted_iota(jnp.int32, (-(-pair_count // 16) * 16, rows), 0)
    pack = jnp.zeros(pack_row.shape, jnp.int32)
    for p in range(pair_count):
        base = bases[p * pieces // pair_count] + CATS * (p % (pair_count // pieces))
        hit = jnp.max(jnp.where(live == base, 1, 0), axis=0, keepdims=True)
        pack = jnp.where(pack_row == p, hit, pack)
    pack = pack.astype(F32).astype(BF16)
    cat_id = lax.broadcasted_iota(jnp.int32, (CATS, rows), 0)
    onehot = jnp.where(cat_id == cat, 1.0, 0.0).astype(BF16)
    side = lax.broadcasted_iota(jnp.int32, (CATS, both), 1) // tile
    own_side = side == lax.broadcasted_iota(jnp.int32, (CATS, both), 0)
    keep = contract_rows(onehot, jnp.where(own_side, 1.0, 0.0).astype(BF16))
    embedded = contract_rows(onehot, table_ref[...])
    query_in = (feats_ref[...].astype(F32) + embedded).astype(BF16)
    query = jnp.dot(query_in, wq_ref[...], preferred_element_type=F32).astype(BF16)
    query = query * jnp.array(0.5 / math.sqrt(head), BF16)
    keep_bf = keep.astype(BF16)
    pair_id = lax.broadcasted_iota(jnp.int32, (pack.shape[0], total_keys), 0)
    key_pair = lax.broadcasted_iota(jnp.int32, (pack.shape[0], total_keys), 1) // BLOCK
    expand = jnp.where(pair_id == key_pair, 1.0, 0.0).astype(BF16)
    mask_ref[...] = contract_rows(pack, expand).astype(BF16)

    lane = lax.broadcasted_iota(jnp.int32, (rows, tile), 1)
    lane_head = lax.broadcasted_iota(jnp.int32, (rows, both), 1) // head % 2
    group = 2
    for t in range(HEADS // 2):
        lanes = slice(t * tile, (t + 1) * tile)
        key_even, key_odd = pair_rows(key_refs, lanes)
        value_even, value_odd = pair_rows(value_refs, lanes)
        values = jnp.concatenate(
            [jnp.concatenate(value_even, axis=0), jnp.concatenate(value_odd, axis=0)], axis=1
        )
        doubled = jnp.concatenate([query[:, lanes]] * CATS, axis=1) * keep_bf
        results = []
        for h in range(2):
            asked = jnp.where(lane_head == h, doubled, jnp.zeros_like(doubled))
            for c in range(0, pair_count, group):
                keys = jnp.concatenate(
                    [
                        jnp.concatenate(key_even[c : c + group], axis=0),
                        jnp.concatenate(key_odd[c : c + group], axis=0),
                    ],
                    axis=1,
                )
                span = slice(c * BLOCK, (c + group) * BLOCK)
                half = contract_lanes(asked, keys)
                weight = (half + half * jnp.tanh(half)).astype(BF16) * mask_ref[:, span]
                weight_ref[h * rows : (h + 1) * rows, span] = weight
            found = jnp.dot(
                weight_ref[h * rows : (h + 1) * rows, :], values, preferred_element_type=F32
            )
            found = found * keep
            results.append(found[:, :tile] + found[:, tile:])
        out_ref[:, lanes] = jnp.where(lane < head, results[0], results[1]).astype(out_ref.dtype)


def finish_kernel(mine_ref, theirs_ref, feats_ref, gain_ref, up_ref, down_ref, out_ref):
    attended = mine_ref[...].astype(F32) + theirs_ref[...].astype(F32)
    mean_square = jnp.mean(attended * attended, axis=-1, keepdims=True)
    normed = (attended * lax.rsqrt(mean_square + 1e-06) * gain_ref[...]).astype(BF16)
    half = 0.5 * jnp.dot(normed, up_ref[...], preferred_element_type=F32)
    hidden = (half + half * jnp.tanh(half)).astype(BF16)
    result = feats_ref[...].astype(F32) + jnp.dot(
        hidden, down_ref[...], preferred_element_type=F32
    )
    out_ref[...] = result.astype(BF16)


def on_chip(kernel, shapes, args, limit, scratch=(), flops=0, keep=True):
    vmem = pl.BlockSpec(memory_space=pltpu.VMEM)
    kind = pltpu.VMEM if keep else jax.ShapeDtypeStruct
    return pl.pallas_call(
        kernel,
        out_shape=[kind(shape, BF16) for shape in shapes],
        in_specs=[vmem] * len(args),
        out_specs=[vmem] * len(shapes),
        scratch_shapes=list(scratch),
        compiler_params=pltpu.CompilerParams(vmem_limit_bytes=limit << 20),
        cost_estimate=pl.CostEstimate(flops=flops, bytes_accessed=1 << 20, transcendentals=0),
    )(*[pltpu.with_memory_space_constraint(arg, pltpu.VMEM) for arg in args])


def shards(
    cand_feats,
    cat_table,
    cand_cat,
    cand_blocks,
    cand_count,
    keys,
    values,
    w_query,
    norm_gain,
    w_up,
    w_down,
):
    rows, width = cand_feats.shape
    blocks_here = keys.shape[0] // BLOCK
    pairs = blocks_here // CATS
    cand_size = lax.axis_size("cand")
    hist_size = lax.axis_size("hist")
    chips = cand_size // CORES

    def moved(array, chip_step, hist_flip):
        route = []
        for place in range(cand_size * hist_size):
            c, z = divmod(place, hist_size)
            route.append((place, (c + CORES * chip_step) % cand_size * hist_size + (z ^ hist_flip)))
        return lax.ppermute(array, ("cand", "hist"), route)

    def swapped(array):
        return lax.ppermute(array, "cand", [(i, i ^ 1) for i in range(cand_size)])

    def first_blocks():
        me, hist = lax.axis_index("cand"), lax.axis_index("hist")
        core = lax.rem(me, CORES)
        return [
            ((me - core + c) * hist_size + hist) * blocks_here for c in (core, 1 - core)
        ]

    asked = (cand_feats, cand_blocks.T, cand_count[None, :])
    away = [[moved(a, s, 0) for a in asked] for s in range(1, chips)]
    keys_far, values_far = swapped(keys), swapped(values)
    own = (keys, values, w_query, cat_table) + asked
    vmem = pl.BlockSpec(memory_space=pltpu.VMEM)
    keys, values, w_query, cat_table, *home = pl.pallas_call(
        start_kernel,
        out_shape=[pltpu.VMEM(array.shape, array.dtype) for array in own],
        in_specs=[pl.BlockSpec(memory_space=pltpu.HBM)] * len(own),
        out_specs=[vmem] * len(own),
        scratch_shapes=[pltpu.SemaphoreType.DMA((len(own),))],
        compiler_params=pltpu.CompilerParams(vmem_limit_bytes=1 << 20),
        cost_estimate=pl.CostEstimate(flops=0, bytes_accessed=2 << 20, transcendentals=0),
        name="start",
    )(*[pltpu.with_memory_space_constraint(array, pltpu.HBM) for array in own])

    def attend(candidates):
        span = CORES * pairs * BLOCK
        return on_chip(
            functools.partial(attend_kernel, first_blocks=first_blocks),
            [(rows, width)],
            (*candidates, cat_table, w_query, keys, keys_far, values, values_far),
            8,
            scratch=(pltpu.VMEM((rows, span), BF16), pltpu.VMEM((2 * rows, span), BF16)),
            flops=8 * rows * span * width,
        )[0]

    def total(arrays):
        return sum(array.astype(F32) for array in arrays).astype(BF16)

    back = [moved(attend(away[s - 1]), chips - s, 0) for s in range(1, chips)]
    partial = total([attend(home)] + back)
    *flips, last = [2**k - 1 for k in range(1, hist_size.bit_length())]
    for flip in flips:
        partial = total([partial, moved(partial, 0, flip)])
    arrived = moved(partial, 0, last)
    return on_chip(
        finish_kernel,
        [(rows, width)],
        (partial, arrived, home[0], norm_gain[None, :], w_up, w_down),
        8,
        flops=4 * rows * width * w_up.shape[1],
        keep=False,
    )[0]


def solution(mesh):
    in_specs = (
        P(("groups", "cand"), None),
        P("groups", None),
        P(("groups", "cand")),
        P(("groups", "cand"), None),
        P(("groups", "cand")),
        P(("groups", "cand", "hist"), None),
        P(("groups", "cand", "hist"), None),
        P(),
        P(),
        P(),
        P(),
    )
    out_specs = P(("groups", "cand"), None)

    return jax.shard_map(shards, mesh=mesh, in_specs=in_specs, out_specs=out_specs, check_vma=False)
```

```python
import functools
import math

import jax
import jax.numpy as jnp
from jax import lax
from jax.experimental import pallas as pl
from jax.experimental.pallas import tpu as pltpu
from jax.sharding import PartitionSpec as P


HEADS = 4
BLOCK = 128
CATS = 2
CORES = 2
PARTS = 1
BF16 = jnp.bfloat16
F32 = jnp.float32


def contract_rows(lhs, rhs):
    return lax.dot_general(lhs, rhs, (((0,), (0,)), ((), ())), preferred_element_type=F32)


def contract_lanes(lhs, rhs):
    return lax.dot_general(lhs, rhs, (((1,), (1,)), ((), ())), preferred_element_type=F32)


def start_kernel(*refs):
    half = len(refs) // 2
    copies = [
        pltpu.make_async_copy(source, target, refs[-1].at[i])
        for i, (source, target) in enumerate(zip(refs[:half], refs[half:]))
    ]
    for copy in copies:
        copy.start()
    for copy in copies:
        copy.wait()


def pack_kernel(lists_ref, count_ref, *out_refs, pairs, first_blocks):
    lists = lists_ref[...]
    cat = lax.rem(lists[:1, :], CATS)
    slot = lax.broadcasted_iota(jnp.int32, lists.shape, 0)
    live = jnp.where(slot < count_ref[...], lists - cat, -CATS)
    row = lax.broadcasted_iota(jnp.int32, out_refs[0].shape, 0)
    for step, out_ref in enumerate(out_refs):
        wanted = first_blocks(step)
        packed = jnp.where(row == len(wanted) * pairs, cat, 0)
        for piece, base in enumerate(wanted):
            for pair in range(pairs):
                hit = jnp.where(live == base + CATS * pair, 1, 0)
                hit = jnp.max(hit, axis=0, keepdims=True)
                packed = jnp.where(row == piece * pairs + pair, hit, packed)
        out_ref[...] = packed.astype(F32).astype(BF16)


def pair_rows(refs, lanes):
    even, odd = [], []
    for ref in refs:
        for start in range(0, ref.shape[0], CATS * BLOCK):
            even.append(ref[start : start + BLOCK, lanes])
            odd.append(ref[start + BLOCK : start + CATS * BLOCK, lanes])
    return even, odd


def attend_kernel(feats_ref, pack_ref, table_ref, wq_ref, *refs, pieces, first_lane):
    key_refs, value_refs = refs[:pieces], refs[pieces : 2 * pieces]
    out_ref, mask_ref, weight_ref = refs[2 * pieces :]
    rows, width = feats_ref.shape
    head = width // HEADS
    tile = 2 * head
    pair_count = mask_ref.shape[1] // BLOCK
    turn_row = lax.broadcasted_iota(jnp.int32, (pack_ref.shape[0], BLOCK), 0)
    turn_lane = lax.broadcasted_iota(jnp.int32, (pack_ref.shape[0], BLOCK), 1)
    columns = contract_rows(
        pack_ref[...], jnp.where(turn_row == turn_lane, 1.0, 0.0).astype(BF16)
    )
    odd = jnp.broadcast_to(columns[:, pair_count : pair_count + 1], (rows, tile)) > 0.5
    query_in = []
    for lane in range(0, width, tile):
        lanes = slice(lane, lane + tile)
        embedded = jnp.where(
            odd, table_ref[1:2, lanes].astype(F32), table_ref[0:1, lanes].astype(F32)
        )
        query_in.append((feats_ref[:, lanes].astype(F32) + embedded).astype(BF16))
    query = jnp.dot(
        jnp.concatenate(query_in, axis=1),
        wq_ref[:, first_lane : first_lane + out_ref.shape[1]],
        preferred_element_type=F32,
    )
    query = query.astype(BF16).astype(F32) * (0.5 / math.sqrt(head))
    for pair in range(pair_count):
        mask_ref[:, pair * BLOCK : (pair + 1) * BLOCK] = jnp.broadcast_to(
            columns[:, pair : pair + 1], (rows, BLOCK)
        ).astype(BF16)

    low = lax.broadcasted_iota(jnp.int32, (rows, tile), 1) < head
    group = 2
    for lane in range(0, out_ref.shape[1], tile):
        lanes = slice(first_lane + lane, first_lane + lane + tile)
        key_even, key_odd = pair_rows(key_refs, lanes)
        value_even, value_odd = pair_rows(value_refs, lanes)
        values = jnp.concatenate(
            [jnp.concatenate(value_even, axis=0), jnp.concatenate(value_odd, axis=0)], axis=1
        )
        mine = query[:, lane : lane + tile]
        asked = []
        for h in range(2):
            part = jnp.where(low == (h == 0), mine, 0.0)
            asked.append(
                jnp.concatenate([jnp.where(odd, 0.0, part), jnp.where(odd, part, 0.0)], axis=1)
            )
        asked = jnp.concatenate(asked, axis=0).astype(BF16)
        for c in range(0, pair_count, group):
            keys = jnp.concatenate(
                [
                    jnp.concatenate(key_even[c : c + group], axis=0),
                    jnp.concatenate(key_odd[c : c + group], axis=0),
                ],
                axis=1,
            )
            span = slice(c * BLOCK, (c + group) * BLOCK)
            half = contract_lanes(asked, keys)
            weight = (half + half * jnp.tanh(half)).astype(BF16)
            mask = mask_ref[:, span]
            weight_ref[:, span] = weight * jnp.concatenate([mask, mask], axis=0)
        found = jnp.dot(weight_ref[...], values, preferred_element_type=F32)
        results = [
            jnp.where(odd, both[:, tile:], both[:, :tile])
            for both in (found[:rows], found[rows:])
        ]
        out_ref[:, lane : lane + tile] = jnp.where(low, results[0], results[1]).astype(
            out_ref.dtype
        )


def finish_kernel(mine_ref, theirs_ref, feats_ref, gain_ref, up_ref, down_ref, out_ref):
    attended = mine_ref[...].astype(F32) + theirs_ref[...].astype(F32)
    mean_square = jnp.mean(attended * attended, axis=-1, keepdims=True)
    normed = (attended * lax.rsqrt(mean_square + 1e-06) * gain_ref[...]).astype(BF16)
    half = 0.5 * jnp.dot(normed, up_ref[...], preferred_element_type=F32)
    hidden = (half + half * jnp.tanh(half)).astype(BF16)
    result = feats_ref[...].astype(F32) + jnp.dot(
        hidden, down_ref[...], preferred_element_type=F32
    )
    out_ref[...] = result.astype(BF16)


def on_chip(kernel, shapes, args, limit, scratch=(), flops=0, keep=True):
    vmem = pl.BlockSpec(memory_space=pltpu.VMEM)
    kind = pltpu.VMEM if keep else jax.ShapeDtypeStruct
    return pl.pallas_call(
        kernel,
        out_shape=[kind(shape, BF16) for shape in shapes],
        in_specs=[vmem] * len(args),
        out_specs=[vmem] * len(shapes),
        scratch_shapes=list(scratch),
        compiler_params=pltpu.CompilerParams(vmem_limit_bytes=limit << 20),
        cost_estimate=pl.CostEstimate(flops=flops, bytes_accessed=1 << 20, transcendentals=0),
    )(*[pltpu.with_memory_space_constraint(arg, pltpu.VMEM) for arg in args])


def shards(
    cand_feats,
    cat_table,
    cand_cat,
    cand_blocks,
    cand_count,
    keys,
    values,
    w_query,
    norm_gain,
    w_up,
    w_down,
):
    rows, width = cand_feats.shape
    blocks_here = keys.shape[0] // BLOCK
    pairs = blocks_here // CATS
    cand_size = lax.axis_size("cand")
    hist_size = lax.axis_size("hist")
    chips = cand_size // CORES

    def moved(array, chip_step, hist_flip):
        route = []
        for place in range(cand_size * hist_size):
            c, z = divmod(place, hist_size)
            route.append((place, (c + CORES * chip_step) % cand_size * hist_size + (z ^ hist_flip)))
        return lax.ppermute(array, ("cand", "hist"), route)

    def swapped(array):
        return lax.ppermute(array, "cand", [(i, i ^ 1) for i in range(cand_size)])

    def first_blocks(step):
        me, hist = lax.axis_index("cand"), lax.axis_index("hist")
        core = lax.rem(me, CORES)
        chip = lax.rem(lax.div(me, CORES) + step, chips)
        return [
            ((chip * CORES + c) * hist_size + hist) * blocks_here for c in (core, 1 - core)
        ]

    feats_in = [moved(cand_feats, s, 0) for s in range(1, chips)]
    keys_far, values_far = swapped(keys), swapped(values)
    vmem = pl.BlockSpec(memory_space=pltpu.VMEM)
    packs = pl.pallas_call(
        functools.partial(pack_kernel, pairs=pairs, first_blocks=first_blocks),
        out_shape=[pltpu.VMEM((-(-(CORES * pairs + 1) // 16) * 16, rows), BF16)] * chips,
        in_specs=[vmem] * 2,
        out_specs=[vmem] * chips,
        compiler_params=pltpu.CompilerParams(vmem_limit_bytes=1 << 20),
        name="pack",
    )(
        *[
            pltpu.with_memory_space_constraint(array, pltpu.HBM)
            for array in (cand_blocks.T, cand_count[None, :])
        ]
    )
    packs_in = [moved(packs[s], s, 0) for s in range(1, chips)]
    own = (keys, values, w_query, cat_table, cand_feats)
    keys, values, w_query, cat_table, feats = pl.pallas_call(
        start_kernel,
        out_shape=[pltpu.VMEM(array.shape, array.dtype) for array in own],
        in_specs=[pl.BlockSpec(memory_space=pltpu.HBM)] * len(own),
        out_specs=[vmem] * len(own),
        scratch_shapes=[pltpu.SemaphoreType.DMA((len(own),))],
        compiler_params=pltpu.CompilerParams(vmem_limit_bytes=1 << 20),
        cost_estimate=pl.CostEstimate(flops=0, bytes_accessed=2 << 20, transcendentals=0),
        name="start",
    )(*[pltpu.with_memory_space_constraint(array, pltpu.HBM) for array in own])

    def attend(feats, pack, first_lane, lanes):
        span = CORES * pairs * BLOCK
        return on_chip(
            functools.partial(attend_kernel, pieces=CORES, first_lane=first_lane),
            [(rows, lanes)],
            (feats, pack, cat_table, w_query, keys, keys_far, values, values_far),
            8,
            scratch=(pltpu.VMEM((rows, span), BF16), pltpu.VMEM((2 * rows, span), BF16)),
            flops=8 * rows * span * lanes,
        )[0]

    def total(arrays):
        return sum(array.astype(F32) for array in arrays).astype(BF16)

    part = width // PARTS
    back = []
    for s in range(1, chips):
        pieces = [
            moved(attend(feats_in[s - 1], packs_in[s - 1], p * part, part), chips - s, 0)
            for p in range(PARTS)
        ]
        back.append(jnp.concatenate(pieces, axis=1))
    partial = total([attend(feats, packs[0], 0, width)] + back)
    *flips, last = [2**k - 1 for k in range(1, hist_size.bit_length())]
    for flip in flips:
        partial = total([partial, moved(partial, 0, flip)])
    arrived = moved(partial, 0, last)
    return on_chip(
        finish_kernel,
        [(rows, width)],
        (partial, arrived, feats, norm_gain[None, :], w_up, w_down),
        8,
        flops=4 * rows * width * w_up.shape[1],
        keep=False,
    )[0]


def solution(mesh):
    in_specs = (
        P(("groups", "cand"), None),
        P("groups", None),
        P(("groups", "cand")),
        P(("groups", "cand"), None),
        P(("groups", "cand")),
        P(("groups", "cand", "hist"), None),
        P(("groups", "cand", "hist"), None),
        P(),
        P(),
        P(),
        P(),
    )
    out_specs = P(("groups", "cand"), None)

    return jax.shard_map(shards, mesh=mesh, in_specs=in_specs, out_specs=out_specs, check_vma=False)
```

```python
import functools
import math

import jax
import jax.numpy as jnp
from jax import lax
from jax.experimental import pallas as pl
from jax.experimental.pallas import tpu as pltpu
from jax.sharding import PartitionSpec as P


HEADS = 4
BLOCK = 128
CATS = 2
CORES = 2
BF16 = jnp.bfloat16
F32 = jnp.float32


def contract_rows(lhs, rhs):
    return lax.dot_general(lhs, rhs, (((0,), (0,)), ((), ())), preferred_element_type=F32)


def contract_lanes(lhs, rhs):
    return lax.dot_general(lhs, rhs, (((1,), (1,)), ((), ())), preferred_element_type=F32)


def start_kernel(*refs, pairs, first_blocks, packs):
    held = (len(refs) - packs - 1) // 2
    sources, out_refs, sems = refs[:held], refs[held : held + packs], refs[-1]
    targets = refs[-3:-1] + refs[held + packs : -3]
    lists_ref, count_ref = targets[:2]
    copies = [
        pltpu.make_async_copy(source, target, sems.at[i])
        for i, (source, target) in enumerate(zip(sources, targets))
    ]
    for copy in copies:
        copy.start()
    for copy in copies[:2]:
        copy.wait()
    lists = lists_ref[...]
    cat = lax.rem(lists[:1, :], CATS)
    slot = lax.broadcasted_iota(jnp.int32, lists.shape, 0)
    live = jnp.where(slot < count_ref[...], lists - cat, -CATS)
    row = lax.broadcasted_iota(jnp.int32, out_refs[0].shape, 0)
    for step, out_ref in enumerate(out_refs):
        wanted = first_blocks(step)
        packed = jnp.where(row == len(wanted) * pairs, cat, 0)
        for piece, base in enumerate(wanted):
            for pair in range(pairs):
                hit = jnp.where(live == base + CATS * pair, 1, 0)
                hit = jnp.max(hit, axis=0, keepdims=True)
                packed = jnp.where(row == piece * pairs + pair, hit, packed)
        out_ref[...] = packed.astype(F32).astype(BF16)
    for copy in copies[2:]:
        copy.wait()


def pair_rows(refs, lanes):
    even, odd = [], []
    for ref in refs:
        for start in range(0, ref.shape[0], CATS * BLOCK):
            even.append(ref[start : start + BLOCK, lanes])
            odd.append(ref[start + BLOCK : start + CATS * BLOCK, lanes])
    return even, odd


def attend_kernel(feats_ref, pack_ref, table_ref, wq_ref, *refs, odd_half):
    key_refs, value_refs = refs[:CORES], refs[CORES : 2 * CORES]
    keep_ref, give_ref, mask_ref, weight_ref = refs[2 * CORES :]
    rows, width = feats_ref.shape
    upper = odd_half()
    head = width // HEADS
    tile = 2 * head
    pair_count = mask_ref.shape[1] // BLOCK
    turn_row = lax.broadcasted_iota(jnp.int32, (pack_ref.shape[0], BLOCK), 0)
    turn_lane = lax.broadcasted_iota(jnp.int32, (pack_ref.shape[0], BLOCK), 1)
    columns = contract_rows(
        pack_ref[...], jnp.where(turn_row == turn_lane, 1.0, 0.0).astype(BF16)
    )
    odd = jnp.broadcast_to(columns[:, pair_count : pair_count + 1], (rows, tile)) > 0.5
    query_in = []
    for lane in range(0, width, tile):
        lanes = slice(lane, lane + tile)
        embedded = jnp.where(
            odd, table_ref[1:2, lanes].astype(F32), table_ref[0:1, lanes].astype(F32)
        )
        query_in.append((feats_ref[:, lanes].astype(F32) + embedded).astype(BF16))
    query = jnp.dot(
        jnp.concatenate(query_in, axis=1),
        wq_ref[...],
        preferred_element_type=F32,
    )
    query = query.astype(BF16).astype(F32) * (0.5 / math.sqrt(head))
    for pair in range(pair_count):
        mask_ref[:, pair * BLOCK : (pair + 1) * BLOCK] = jnp.broadcast_to(
            columns[:, pair : pair + 1], (rows, BLOCK)
        ).astype(BF16)

    low = lax.broadcasted_iota(jnp.int32, (rows, tile), 1) < head
    group = 2
    for lane in range(0, width, tile):
        lanes = slice(lane, lane + tile)
        mine = query[:, lanes]
        asked = []
        for h in range(2):
            part = jnp.where(low == (h == 0), mine, 0.0)
            asked.append(
                jnp.concatenate([jnp.where(odd, 0.0, part), jnp.where(odd, part, 0.0)], axis=1)
            )
        asked = jnp.concatenate(asked, axis=0).astype(BF16)
        key_even, key_odd = pair_rows(key_refs, lanes)
        for c in range(0, pair_count, group):
            keys = jnp.concatenate(
                [
                    jnp.concatenate(key_even[c : c + group], axis=0),
                    jnp.concatenate(key_odd[c : c + group], axis=0),
                ],
                axis=1,
            )
            span = slice(c * BLOCK, (c + group) * BLOCK)
            half = contract_lanes(asked, keys)
            weight = (half + half * jnp.tanh(half)).astype(BF16)
            mask = mask_ref[:, span]
            weight_ref[:, span] = weight * jnp.concatenate([mask, mask], axis=0)
        value_even, value_odd = pair_rows(value_refs, lanes)
        values = jnp.concatenate(
            [jnp.concatenate(value_even, axis=0), jnp.concatenate(value_odd, axis=0)], axis=1
        )
        found = jnp.dot(weight_ref[...], values, preferred_element_type=F32)
        results = [
            jnp.where(odd, both[:, tile:], both[:, :tile])
            for both in (found[:rows], found[rows:])
        ]
        result = jnp.where(low, results[0], results[1]).astype(BF16)
        first, second = result[: rows // 2], result[rows // 2 :]
        keep_ref[:, lanes] = jnp.where(upper, second, first)
        give_ref[:, lanes] = jnp.where(upper, first, second)


def finish_kernel(*refs, odd_half):
    kept_ref, near_ref, far_ref, across_ref, feats_ref, gain_ref, up_ref, down_ref = refs[:8]
    out_ref, done_ref, sems = refs[8:]
    upper = odd_half()
    kept = kept_ref[...].astype(F32) + far_ref[...].astype(F32)
    given = near_ref[...].astype(F32) + across_ref[...].astype(F32)
    half_rows = kept.shape[0]
    copies = []
    for i in range(2):
        rows = slice(i * half_rows, (i + 1) * half_rows)
        attended = jnp.where(upper == (i == 1), kept, given)
        mean_square = jnp.mean(attended * attended, axis=-1, keepdims=True)
        normed = (attended * lax.rsqrt(mean_square + 1e-06) * gain_ref[...]).astype(BF16)
        half = 0.5 * jnp.dot(normed, up_ref[...], preferred_element_type=F32)
        hidden = (half + half * jnp.tanh(half)).astype(BF16)
        result = feats_ref[rows, :].astype(F32) + jnp.dot(
            hidden, down_ref[...], preferred_element_type=F32
        )
        done_ref[rows, :] = result.astype(BF16)
        copies.append(pltpu.make_async_copy(done_ref.at[rows], out_ref.at[rows], sems.at[i]))
        copies[-1].start()
    for copy in copies:
        copy.wait()


def on_chip(kernel, shapes, args, limit, scratch=(), flops=0, kind=pltpu.VMEM):
    return pl.pallas_call(
        kernel,
        out_shape=[kind(shape, BF16) for shape in shapes],
        in_specs=[pl.BlockSpec(memory_space=pltpu.VMEM)] * len(args),
        out_specs=[pl.BlockSpec(memory_space=kind)] * len(shapes),
        scratch_shapes=list(scratch),
        compiler_params=pltpu.CompilerParams(vmem_limit_bytes=limit << 20),
        cost_estimate=pl.CostEstimate(flops=flops, bytes_accessed=1 << 20, transcendentals=0),
    )(*[pltpu.with_memory_space_constraint(arg, pltpu.VMEM) for arg in args])


def total(arrays):
    return sum(array.astype(F32) for array in arrays).astype(BF16)


def shards(
    cand_feats,
    cat_table,
    cand_cat,
    cand_blocks,
    cand_count,
    keys,
    values,
    w_query,
    norm_gain,
    w_up,
    w_down,
):
    rows, width = cand_feats.shape
    blocks_here = keys.shape[0] // BLOCK
    pairs = blocks_here // CATS
    cand_size = lax.axis_size("cand")
    hist_size = lax.axis_size("hist")
    chips = cand_size // CORES

    def moved(array, chip_step, hist_flip):
        route = []
        for place in range(cand_size * hist_size):
            c, z = divmod(place, hist_size)
            route.append((place, (c + CORES * chip_step) % cand_size * hist_size + (z ^ hist_flip)))
        return lax.ppermute(array, ("cand", "hist"), route)

    def swapped(array):
        return lax.ppermute(array, "cand", [(i, i ^ 1) for i in range(cand_size)])

    def first_blocks(step):
        me, hist = lax.axis_index("cand"), lax.axis_index("hist")
        core = lax.rem(me, CORES)
        chip = lax.rem(lax.div(me, CORES) + step, chips)
        return [
            ((chip * CORES + c) * hist_size + hist) * blocks_here for c in (1 - core, core)
        ]

    def odd_half():
        return lax.rem(lax.axis_index("hist"), 2) == 1

    feats_in = [moved(cand_feats, s, 0) for s in range(1, chips)]
    keys_far, values_far = swapped(keys), swapped(values)
    vmem, hbm = pl.BlockSpec(memory_space=pltpu.VMEM), pl.BlockSpec(memory_space=pltpu.HBM)
    rows_in = (cand_blocks.T, cand_count[None, :])
    own = (cand_feats, cat_table, w_query, keys, values)
    *packs, feats, cat_table, w_query, keys, values = pl.pallas_call(
        functools.partial(start_kernel, pairs=pairs, first_blocks=first_blocks, packs=chips),
        out_shape=[pltpu.VMEM((-(-(CORES * pairs + 1) // 16) * 16, rows), BF16)] * chips
        + [pltpu.VMEM(array.shape, array.dtype) for array in own],
        in_specs=[hbm] * (len(rows_in) + len(own)),
        out_specs=[vmem] * (chips + len(own)),
        scratch_shapes=[pltpu.VMEM(array.shape, array.dtype) for array in rows_in]
        + [pltpu.SemaphoreType.DMA((len(rows_in) + len(own),))],
        compiler_params=pltpu.CompilerParams(vmem_limit_bytes=1 << 20),
        name="start",
    )(*[pltpu.with_memory_space_constraint(array, pltpu.HBM) for array in rows_in + own])
    packs_in = [moved(packs[s], s, 0) for s in range(1, chips)]

    def attend(feats, pack):
        span = CORES * pairs * BLOCK
        return on_chip(
            functools.partial(attend_kernel, odd_half=odd_half),
            [(rows // 2, width)] * 2,
            (feats, pack, cat_table, w_query, keys_far, keys, values_far, values),
            8,
            scratch=(pltpu.VMEM((rows, span), BF16), pltpu.VMEM((2 * rows, span), BF16)),
            flops=8 * rows * span * width,
        )

    keep, give = attend(feats, packs[0])
    halves = [keep, moved(give, 0, 1)]
    for s in range(1, chips):
        keep, give = attend(feats_in[s - 1], packs_in[s - 1])
        halves.append(moved(give, chips - s, 1))
        halves.append(moved(keep, chips - s, 0))
    kept = total(halves)
    for k in range(2, hist_size.bit_length() - 1):
        kept = total([kept, moved(kept, 0, 2**k)])
    across = moved(kept, 0, 3)
    far = moved(kept, 0, 2)
    near = moved(kept, 0, 1)
    return on_chip(
        functools.partial(finish_kernel, odd_half=odd_half),
        [(rows, width)],
        (kept, near, far, across, feats, norm_gain[None, :], w_up, w_down),
        8,
        scratch=(pltpu.VMEM((rows, width), BF16), pltpu.SemaphoreType.DMA((2,))),
        flops=4 * rows * width * w_up.shape[1],
        kind=pltpu.HBM,
    )[0]


def solution(mesh):
    in_specs = (
        P(("groups", "cand"), None),
        P("groups", None),
        P(("groups", "cand")),
        P(("groups", "cand"), None),
        P(("groups", "cand")),
        P(("groups", "cand", "hist"), None),
        P(("groups", "cand", "hist"), None),
        P(),
        P(),
        P(),
        P(),
    )
    out_specs = P(("groups", "cand"), None)

    return jax.shard_map(shards, mesh=mesh, in_specs=in_specs, out_specs=out_specs, check_vma=False)
```

```python
import functools
import math

import jax
import jax.numpy as jnp
from jax import lax
from jax.experimental import pallas as pl
from jax.experimental.pallas import tpu as pltpu
from jax.sharding import PartitionSpec as P


HEADS = 4
BLOCK = 128
CATS = 2
CORES = 2
BF16 = jnp.bfloat16
F32 = jnp.float32


def contract_rows(lhs, rhs):
    return lax.dot_general(lhs, rhs, (((0,), (0,)), ((), ())), preferred_element_type=F32)


def contract_lanes(lhs, rhs):
    return lax.dot_general(lhs, rhs, (((1,), (1,)), ((), ())), preferred_element_type=F32)


def start_kernel(*refs, pairs, first_blocks, packs):
    held = (len(refs) - packs - 1) // 2
    sources, out_refs, sems = refs[:held], refs[held : held + packs], refs[-1]
    targets = refs[-3:-1] + refs[held + packs : -3]
    lists_ref, count_ref = targets[:2]
    copies = [
        pltpu.make_async_copy(source, target, sems.at[i])
        for i, (source, target) in enumerate(zip(sources, targets))
    ]
    for copy in copies:
        copy.start()
    for copy in copies[:2]:
        copy.wait()
    lists = lists_ref[...]
    cat = lax.rem(lists[:1, :], CATS)
    slot = lax.broadcasted_iota(jnp.int32, lists.shape, 0)
    live = jnp.where(slot < count_ref[...], lists - cat, -CATS)
    row = lax.broadcasted_iota(jnp.int32, out_refs[0].shape, 0)
    for step, out_ref in enumerate(out_refs):
        wanted = first_blocks(step)
        packed = jnp.where(row == len(wanted) * pairs, cat, 0)
        for piece, base in enumerate(wanted):
            for pair in range(pairs):
                hit = jnp.where(live == base + CATS * pair, 1, 0)
                hit = jnp.max(hit, axis=0, keepdims=True)
                packed = jnp.where(row == piece * pairs + pair, hit, packed)
        out_ref[...] = packed.astype(F32).astype(BF16)
    for copy in copies[2:]:
        copy.wait()


def pair_rows(refs, lanes):
    even, odd = [], []
    for ref in refs:
        for start in range(0, ref.shape[0], CATS * BLOCK):
            even.append(ref[start : start + BLOCK, lanes])
            odd.append(ref[start + BLOCK : start + CATS * BLOCK, lanes])
    return even, odd


def attend_kernel(feats_ref, pack_ref, table_ref, wq_ref, *refs, odd_half):
    key_refs, value_refs = refs[:CORES], refs[CORES : 2 * CORES]
    keep_ref, give_ref, mask_ref, weight_ref = refs[2 * CORES :]
    rows, width = feats_ref.shape
    upper = odd_half()
    head = width // HEADS
    tile = 2 * head
    pair_count = mask_ref.shape[1] // BLOCK
    turn_row = lax.broadcasted_iota(jnp.int32, (pack_ref.shape[0], BLOCK), 0)
    turn_lane = lax.broadcasted_iota(jnp.int32, (pack_ref.shape[0], BLOCK), 1)
    columns = contract_rows(
        pack_ref[...], jnp.where(turn_row == turn_lane, 1.0, 0.0).astype(BF16)
    )
    listed = columns.astype(BF16)
    odd = jnp.broadcast_to(columns[:, pair_count : pair_count + 1], (rows, tile)) > 0.5
    query_in = []
    for lane in range(0, width, tile):
        lanes = slice(lane, lane + tile)
        embedded = jnp.where(
            odd, table_ref[1:2, lanes].astype(F32), table_ref[0:1, lanes].astype(F32)
        )
        query_in.append((feats_ref[:, lanes].astype(F32) + embedded).astype(BF16))
    query = jnp.dot(
        jnp.concatenate(query_in, axis=1),
        wq_ref[...],
        preferred_element_type=F32,
    )
    query = query.astype(BF16).astype(F32) * (0.5 / math.sqrt(head))
    low = lax.broadcasted_iota(jnp.int32, (rows, tile), 1) < head
    group = 2
    for lane in range(0, width, tile):
        lanes = slice(lane, lane + tile)
        mine = query[:, lanes]
        asked = []
        for h in range(2):
            part = jnp.where(low == (h == 0), mine, 0.0)
            asked.append(
                jnp.concatenate([jnp.where(odd, 0.0, part), jnp.where(odd, part, 0.0)], axis=1)
            )
        asked = jnp.concatenate(asked, axis=0).astype(BF16)
        key_even, key_odd = pair_rows(key_refs, lanes)
        for c in range(0, pair_count, group):
            keys = jnp.concatenate(
                [
                    jnp.concatenate(key_even[c : c + group], axis=0),
                    jnp.concatenate(key_odd[c : c + group], axis=0),
                ],
                axis=1,
            )
            span = slice(c * BLOCK, (c + group) * BLOCK)
            half = contract_lanes(asked, keys)
            weight = (half + half * jnp.tanh(half)).astype(BF16)
            if lane == 0:
                for pair in range(c, c + group):
                    mask_ref[:, pair * BLOCK : (pair + 1) * BLOCK] = jnp.broadcast_to(
                        listed[:, pair : pair + 1], (rows, BLOCK)
                    )
            mask = mask_ref[:, span]
            weight_ref[:, span] = weight * jnp.concatenate([mask, mask], axis=0)
        value_even, value_odd = pair_rows(value_refs, lanes)
        values = jnp.concatenate(
            [jnp.concatenate(value_even, axis=0), jnp.concatenate(value_odd, axis=0)], axis=1
        )
        found = jnp.dot(weight_ref[...], values, preferred_element_type=F32)
        results = [
            jnp.where(odd, both[:, tile:], both[:, :tile])
            for both in (found[:rows], found[rows:])
        ]
        result = jnp.where(low, results[0], results[1]).astype(BF16)
        first, second = result[: rows // 2], result[rows // 2 :]
        keep_ref[:, lanes] = jnp.where(upper, second, first)
        give_ref[:, lanes] = jnp.where(upper, first, second)


def finish_kernel(one_ref, two_ref, feats_ref, gain_ref, up_ref, down_ref, *refs, upper):
    out_ref, done_ref, sem = refs[-3:]
    half_rows = one_ref.shape[0]
    rows = pl.ds(pl.multiple_of(upper() * half_rows, half_rows), half_rows)
    attended = one_ref[...].astype(F32) + two_ref[...].astype(F32)
    mean_square = jnp.mean(attended * attended, axis=-1, keepdims=True)
    normed = (attended * lax.rsqrt(mean_square + 1e-06) * gain_ref[...]).astype(BF16)
    half = 0.5 * jnp.dot(normed, up_ref[...], preferred_element_type=F32)
    hidden = (half + half * jnp.tanh(half)).astype(BF16)
    result = feats_ref[rows, :].astype(F32) + jnp.dot(
        hidden, down_ref[...], preferred_element_type=F32
    )
    done_ref[...] = result.astype(BF16)
    copy = pltpu.make_async_copy(done_ref, out_ref.at[rows], sem)
    copy.start()
    copy.wait()


def on_chip(kernel, shapes, args, limit, scratch=(), flops=0, kind=pltpu.VMEM, held=(), alias=None):
    return pl.pallas_call(
        kernel,
        out_shape=[kind(shape, BF16) for shape in shapes],
        in_specs=[pl.BlockSpec(memory_space=pltpu.VMEM)] * len(args)
        + [pl.BlockSpec(memory_space=pltpu.HBM)] * len(held),
        input_output_aliases=alias or {},
        out_specs=[pl.BlockSpec(memory_space=kind)] * len(shapes),
        scratch_shapes=list(scratch),
        compiler_params=pltpu.CompilerParams(vmem_limit_bytes=limit << 20),
        cost_estimate=pl.CostEstimate(flops=flops, bytes_accessed=1 << 20, transcendentals=0),
    )(
        *[pltpu.with_memory_space_constraint(arg, pltpu.VMEM) for arg in args],
        *[pltpu.with_memory_space_constraint(arg, pltpu.HBM) for arg in held],
    )


def total(arrays):
    return sum(array.astype(F32) for array in arrays).astype(BF16)


def shards(
    cand_feats,
    cat_table,
    cand_cat,
    cand_blocks,
    cand_count,
    keys,
    values,
    w_query,
    norm_gain,
    w_up,
    w_down,
):
    rows, width = cand_feats.shape
    blocks_here = keys.shape[0] // BLOCK
    pairs = blocks_here // CATS
    cand_size = lax.axis_size("cand")
    hist_size = lax.axis_size("hist")
    chips = cand_size // CORES

    def moved(array, chip_step, hist_flip):
        route = []
        for place in range(cand_size * hist_size):
            c, z = divmod(place, hist_size)
            route.append((place, (c + CORES * chip_step) % cand_size * hist_size + (z ^ hist_flip)))
        return lax.ppermute(array, ("cand", "hist"), route)

    def shifted(array, step):
        return lax.ppermute(
            array, "hist", [(z, z // 4 * 4 + (z + step) % 4) for z in range(hist_size)]
        )

    def swapped(array):
        return lax.ppermute(array, "cand", [(i, i ^ 1) for i in range(cand_size)])

    def first_blocks(step):
        me, hist = lax.axis_index("cand"), lax.axis_index("hist")
        core = lax.rem(me, CORES)
        chip = lax.rem(lax.div(me, CORES) + step, chips)
        return [
            ((chip * CORES + c) * hist_size + hist) * blocks_here for c in (1 - core, core)
        ]

    def odd_half():
        return lax.rem(lax.axis_index("hist"), 2) == 1

    feats_in = [moved(cand_feats, s, 0) for s in range(1, chips)]
    keys_far, values_far = swapped(keys), swapped(values)
    vmem, hbm = pl.BlockSpec(memory_space=pltpu.VMEM), pl.BlockSpec(memory_space=pltpu.HBM)
    rows_in = (cand_blocks.T, cand_count[None, :])
    own = (cand_feats, cat_table, w_query, keys, values)
    *packs, feats, cat_table, w_query, keys, values = pl.pallas_call(
        functools.partial(start_kernel, pairs=pairs, first_blocks=first_blocks, packs=chips),
        out_shape=[pltpu.VMEM((-(-(CORES * pairs + 1) // 16) * 16, rows), BF16)] * chips
        + [pltpu.VMEM(array.shape, array.dtype) for array in own],
        in_specs=[hbm] * (len(rows_in) + len(own)),
        out_specs=[vmem] * (chips + len(own)),
        scratch_shapes=[pltpu.VMEM(array.shape, array.dtype) for array in rows_in]
        + [pltpu.SemaphoreType.DMA((len(rows_in) + len(own),))],
        compiler_params=pltpu.CompilerParams(vmem_limit_bytes=1 << 20),
        name="start",
    )(*[pltpu.with_memory_space_constraint(array, pltpu.HBM) for array in rows_in + own])
    packs_in = [moved(packs[s], s, 0) for s in range(1, chips)]

    def attend(feats, pack):
        span = CORES * pairs * BLOCK
        return on_chip(
            functools.partial(attend_kernel, odd_half=odd_half),
            [(rows // 2, width)] * 2,
            (feats, pack, cat_table, w_query, keys_far, keys, values_far, values),
            8,
            scratch=(pltpu.VMEM((rows, span), BF16), pltpu.VMEM((2 * rows, span), BF16)),
            flops=8 * rows * span * width,
        )

    keep, give = attend(feats, packs[0])
    halves = [keep, moved(give, 0, 1)]
    for s in range(1, chips):
        keep, give = attend(feats_in[s - 1], packs_in[s - 1])
        halves.append(moved(give, chips - s, 1))
        halves.append(moved(keep, chips - s, 0))
    kept = total(halves)
    for k in range(2, hist_size.bit_length() - 1):
        kept = total([kept, moved(kept, 0, 2**k)])
    far = moved(kept, 0, 2)
    across = shifted(kept, 1)
    near = shifted(kept, 3)

    def finish(one, two, given, held=()):
        args = (one, two, feats, norm_gain[None, :], w_up, w_down)
        return on_chip(
            functools.partial(
                finish_kernel, upper=lambda: lax.rem(lax.axis_index("hist") + given, 2)
            ),
            [(rows, width)],
            args,
            8,
            scratch=(pltpu.VMEM((rows // 2, width), BF16), pltpu.SemaphoreType.DMA),
            flops=2 * rows * width * w_up.shape[1],
            kind=pltpu.HBM,
            held=held,
            alias={len(args): 0} if held else {},
        )[0]

    return finish(near, across, 1, (finish(kept, far, 0),))


def solution(mesh):
    in_specs = (
        P(("groups", "cand"), None),
        P("groups", None),
        P(("groups", "cand")),
        P(("groups", "cand"), None),
        P(("groups", "cand")),
        P(("groups", "cand", "hist"), None),
        P(("groups", "cand", "hist"), None),
        P(),
        P(),
        P(),
        P(),
    )
    out_specs = P(("groups", "cand"), None)

    return jax.shard_map(shards, mesh=mesh, in_specs=in_specs, out_specs=out_specs, check_vma=False)
```
